256 devices in a mesh: loop: 16 (over z, y_lo), rep: 16 (over y_hi, x, core).
Axes of the slice: x: 4, y: 4 (y_hi: 2, y_lo: 2; y = y_hi * 2 + y_lo), z: 8, core: 2. Of those that a mesh axis runs over, the one named last changes fastest.
Arguments:
- features: bfloat16 [65536, 128], P(('loop', 'rep')), may hold values from -6 to 6
- w_self: bfloat16 [128, 256], replicated, may hold values from -0.5 to 0.5
- w_neigh: bfloat16 [128, 256], replicated, may hold values from -0.5 to 0.5
- bias: float32 [256], replicated, may hold values from -3 to 3
- degree: int32 [65536], P(('loop', 'rep')), may hold values from 1 to 4
- tiles: bfloat16 [16, 16, 16, 16, 128, 128], P('loop', 'rep'), may hold values from -0.0625 to 0.0625
- dst_block: int32 [16, 16, 16, 16], P('loop', 'rep'), may hold values from 0 to 31, as said below
- src_block: int32 [16, 16, 16, 16], P('loop', 'rep'), may hold values from 0 to 1, as said below
- live_count: int32 [16, 16, 16], P('loop', 'rep'), may hold values from 1 to 16, as said below
- cotangent: bfloat16 [65536, 256], P(('loop', 'rep')), may hold values from -6 to 6
Outputs:
- output: bfloat16 [65536, 256], P(('loop', 'rep'))
- grad_input: bfloat16 [65536, 128], P(('loop', 'rep'))
- grad_self: float32 [128, 256], replicated
- grad_neigh: float32 [128, 256], replicated
- grad_bias: float32 [256], replicated
The draws below stay inside these ranges and needn't reach their ends.
Inputs may be any that keep to these rules, and one draw needn't show every extreme that they name: Within one (p, r, q) the 16 slots name distinct pairs (dst_block, src_block). Within one (p, r, q) the 16 slots name distinct pairs (dst_block, src_block). `live_count`: every device (p, r) has some q with all 16 slots live; slots at or past the count hold tiles that are not part of the graph.
All inputs are finite; a program needn't handle non-finite values.
Results may differ from the reference program's by a relative error of at most 0.0075.
Values may be sent and summed in bfloat16 or wider, within the bound.
A program may use at most 128 MiB of HBM per device.

```python
import math
import jax
import jax.numpy as jnp
from jax import lax

F = 128
H = 256
BLK = 128
SLOTS = 16
SUB_BLK = 2
NODES = 65536
N_LOOP = 16
N_REP = 16


def tile_pairs(key):
    base = jax.random.fold_in(key, 7)
    keys = jax.random.split(base, N_LOOP * N_REP * N_LOOP)
    candidates = SUB_BLK * SUB_BLK * N_REP
    picks = jax.vmap(lambda one_key: jax.random.permutation(one_key, candidates)[:SLOTS])(keys)
    return picks.reshape(N_LOOP, N_REP, N_LOOP, SLOTS).astype(jnp.int32)


def draw_dst_block(key, part):
    return tile_pairs(key) // SUB_BLK


def draw_src_block(key, part):
    return tile_pairs(key) % SUB_BLK


def draw_live_count(key, part):
    base = jax.random.fold_in(key, 11)
    key_level, key_raw, key_full = jax.random.split(base, 3)
    level = jax.random.randint(key_level, (N_LOOP, N_REP, 1), 1, SLOTS + 1)
    raw_counts = jax.random.randint(key_raw, (N_LOOP, N_REP, N_LOOP), 0, SLOTS * 4)
    counts = 1 + raw_counts % level
    full_part = jax.random.randint(key_full, (N_LOOP, N_REP, 1), 0, N_LOOP)
    positions = jnp.arange(N_LOOP)[None, None, :]
    return jnp.where(positions == full_part, SLOTS, counts).astype(jnp.int32)


def plant(array, own_key, low, top_value):
    index_at = [jax.random.randint(jax.random.fold_in(own_key, axis), (), 0, length) for axis, length in enumerate(array.shape)]
    main_axis = array.shape.index(max(array.shape))
    neighbour = index_at[:main_axis] + [(index_at[main_axis] + 1) % array.shape[main_axis]] + index_at[main_axis + 1:]
    return array.at[tuple(index_at)].set(low).at[tuple(neighbour)].set(top_value)


def levels(stream_key, dims, shards, low, top_value):
    factor_of = 1.0
    for dim, blocks in shards:
        steps = jax.random.uniform(jax.random.fold_in(jax.random.fold_in(stream_key, 6), dim), (blocks,), jnp.float32, low / len(shards), top_value / len(shards))
        factor_of = factor_of * jnp.repeat(jnp.exp(steps), dims[dim] // blocks).reshape((-1,) + (1,) * (len(dims) - 1 - dim))
    return factor_of


def bell_draw(key, extent, scale, limit, pieces=(), kind=jnp.bfloat16):
    drawn = jax.random.normal(key, extent, jnp.float32) * scale
    if len(pieces) > 0:
        drawn = levels(key, extent, pieces, -0.22, 0.18) * drawn
    return jnp.clip(drawn, min=-limit, max=limit).astype(kind)


def setup_inputs(seed: int = 0) -> dict:
    splits = jax.random.split(jax.random.key(seed), 11)
    features = bell_draw(splits[0], (NODES, F), 1.0, 6.0, ((0, 256),))
    w_self = bell_draw(splits[1], (F, H), F ** -0.5, 0.5)
    w_neigh = bell_draw(splits[2], (F, H), F ** -0.5, 0.5)
    bias = bell_draw(splits[3], (H,), 0.5, 3.0, (), jnp.float32)
    degree = plant(jax.random.randint(splits[4], (NODES,), 1, 5), jax.random.fold_in(splits[4], 1), 1, 4).astype(jnp.int32)
    tiles = bell_draw(splits[5], (N_LOOP, N_REP, N_LOOP, SLOTS, BLK, BLK), (BLK * N_LOOP * SLOTS // 4) ** -0.5, 0.0625, ((0, 16), (1, 16)))
    dst_block = draw_dst_block(jax.random.fold_in(splits[10], 71), 0)
    src_block = draw_src_block(jax.random.fold_in(splits[10], 71), 0)
    live_count = draw_live_count(jax.random.fold_in(splits[10], 71), 0)
    cotangent = bell_draw(splits[9], (NODES, H), 1.0, 6.0, ((0, 256),))
    return dict(features=features, w_self=w_self, w_neigh=w_neigh, bias=bias, degree=degree, tiles=tiles, dst_block=dst_block, src_block=src_block, live_count=live_count, cotangent=cotangent)


def reference(features, w_self, w_neigh, bias, degree, tiles, dst_block, src_block, live_count, cotangent):
    row_blocks = SUB_BLK * N_REP
    part_rows = row_blocks * BLK
    blocks = features.reshape(N_LOOP, N_REP, SUB_BLK, BLK, F)
    part_index = jnp.arange(N_LOOP)[None, :, None]
    rep_index = jnp.arange(N_REP)[:, None, None]
    slot_index = jnp.arange(SLOTS)[None, None, :]

    def forward_part(owner):
        tile_owner = tiles[owner].astype(jnp.float32)
        dst_owner = dst_block[owner]
        src_owner = src_block[owner]
        live_mask = (slot_index < live_count[owner][:, :, None]).astype(jnp.float32)
        chosen = blocks[part_index, rep_index, src_owner].astype(jnp.float32)
        product = jnp.einsum('rqtij,rqtjf->rqtif', tile_owner, chosen) * live_mask[..., None, None]
        summed = jax.ops.segment_sum(product.reshape(-1, BLK, F), dst_owner.reshape(-1), num_segments=row_blocks)
        return summed.reshape(part_rows, F)
    agg_sum = lax.map(forward_part, jnp.arange(N_LOOP)).reshape(NODES, F)
    degree_f = degree.astype(jnp.float32)[:, None]
    aggregate = (agg_sum / degree_f).astype(jnp.bfloat16)
    preact = jnp.dot(features, w_self, preferred_element_type=jnp.float32) + jnp.dot(aggregate, w_neigh, preferred_element_type=jnp.float32) + bias
    sigmoid_val = jax.nn.sigmoid(preact)
    output = (preact * sigmoid_val).astype(jnp.bfloat16)
    grad_pre = (cotangent.astype(jnp.float32) * sigmoid_val * (1.0 + preact * (1.0 - sigmoid_val))).astype(jnp.bfloat16)
    grad_scale = 1.0 / math.sqrt(NODES)
    grad_self = jnp.dot(features.T, grad_pre, preferred_element_type=jnp.float32) * grad_scale
    grad_neigh = jnp.dot(aggregate.T, grad_pre, preferred_element_type=jnp.float32) * grad_scale
    grad_bias = lax.optimization_barrier(jnp.sum(grad_pre.astype(jnp.float32), axis=0)) * grad_scale
    grad_agg = (jnp.dot(grad_pre, w_neigh.T, preferred_element_type=jnp.float32) / degree_f).astype(jnp.bfloat16)
    grad_blocks = grad_agg.reshape(N_LOOP, row_blocks, BLK, F)

    def backward_part(running, owner):
        tile_owner = tiles[owner].astype(jnp.float32)
        dst_owner = dst_block[owner]
        src_owner = src_block[owner]
        live_mask = (slot_index < live_count[owner][:, :, None]).astype(jnp.float32)
        chosen = grad_blocks[owner][dst_owner].astype(jnp.float32)
        product = jnp.einsum('rqtij,rqtif->rqtjf', tile_owner, chosen) * live_mask[..., None, None]
        running = running.at[part_index, rep_index, src_owner].add(product)
        return (running, None)
    start = jnp.zeros((N_LOOP, N_REP, SUB_BLK, BLK, F), jnp.float32)
    neigh_grad, _ = lax.scan(backward_part, start, jnp.arange(N_LOOP))
    self_grad = jnp.dot(grad_pre, w_self.T, preferred_element_type=jnp.float32)
    grad_input = (self_grad + neigh_grad.reshape(NODES, F)).astype(jnp.bfloat16)
    return (output, grad_input, grad_self, grad_neigh, grad_bias)
```

```python
import math

import jax
import jax.numpy as jnp
from jax import lax
from jax.experimental import pallas as pl
from jax.experimental.pallas import tpu as pltpu
from jax.sharding import PartitionSpec as P

F32 = jnp.float32
BF16 = jnp.bfloat16
MESH = pl.DeviceIdType.MESH
Z = 8
X = 4
CHIP_STEPS = ((1, 2), (1, 1), (1, 3), (0, 2), (1, 0), (0, 1), (0, 3))


def remote(src, dst, send_sem, recv_sem, device):
    return pltpu.make_async_remote_copy(
        src_ref=src,
        dst_ref=dst,
        send_sem=send_sem,
        recv_sem=recv_sem,
        device_id=device,
        device_id_type=MESH,
    )


def loop_node(dz, col):
    here = lax.axis_index("loop")
    z = lax.rem(here // 2 + (dz + Z), Z)
    return z * 2 + lax.rem(here % 2 + col, 2)


def chip_node(dy, dx):
    chip = lax.axis_index("rep") // 2
    return lax.rem(chip // X + dy, 2) * X + lax.rem(chip % X + dx, X)


def gather_kernel(x_ref, g_ref, own_sem, pair_sem, send_sem, recv_sem):
    rep = lax.axis_index("rep")
    half = x_ref.shape[0] // 2
    barrier = pltpu.get_barrier_semaphore()
    for dz, col in ((1, 0), (-1, 0), (0, 1)):
        pl.semaphore_signal(
            barrier, inc=1, device_id=(loop_node(dz, col), rep), device_id_type=MESH
        )
    pl.semaphore_wait(barrier, 3)
    own = pltpu.make_async_copy(x_ref, g_ref.at[loop_node(0, 0)], own_sem)
    own.start()

    def hop(way, col, k):
        sign = 1 - 2 * way
        origin = loop_node(-sign * (k - 1), col)
        src = x_ref if (k == 1 and col == 0) else g_ref.at[origin]
        dst = g_ref.at[origin]
        if k == Z // 2:
            rows = pl.ds(way * half, half)
            src, dst = src.at[rows], dst.at[rows]
        return remote(
            src,
            dst,
            send_sem.at[way, col, k - 1],
            recv_sem.at[way, col, k - 1],
            (loop_node(sign, 0), rep),
        )

    def arrival(way, col, k):
        sign = 1 - 2 * way
        dst = g_ref.at[loop_node(-sign * k, col)]
        if k == Z // 2:
            dst = dst.at[pl.ds(way * half, half)]
        return remote(
            dst,
            dst,
            send_sem.at[way, col, k - 1],
            recv_sem.at[way, col, k - 1],
            (loop_node(sign, 0), rep),
        )

    pair = remote(
        x_ref, g_ref.at[loop_node(0, 0)], pair_sem.at[0], pair_sem.at[1], (loop_node(0, 1), rep)
    )
    pair.start()
    sent = []

    def send(way, col, k):
        copy = hop(way, col, k)
        copy.start()
        sent.append(copy)

    send(0, 0, 1)
    send(1, 0, 1)
    pair_in = remote(
        x_ref, g_ref.at[loop_node(0, 1)], pair_sem.at[0], pair_sem.at[1], (loop_node(0, 1), rep)
    )
    pair_in.wait_recv()
    send(0, 1, 1)
    send(1, 1, 1)
    for k in range(1, Z // 2):
        for col in (0, 1):
            for way in (0, 1):
                arrival(way, col, k).wait_recv()
                send(way, col, k + 1)
    for col in (0, 1):
        for way in (0, 1):
            arrival(way, col, Z // 2).wait_recv()
    pair.wait_send()
    for copy in sent:
        copy.wait_send()
    own.wait()


def product_kernel(dst_ref, src_ref, live_ref, g_ref, tile_ref, out_ref, tile_vmem, acc, sems):
    sources, depth, width = tile_ref.shape
    blk = width
    slots = depth // blk
    blocks = acc.shape[0] - 1

    def fetch(q):
        return pltpu.make_async_copy(tile_ref.at[q], tile_vmem.at[q], sems.at[q])

    for q in range(sources):
        fetch(q).start()
    acc[...] = jnp.zeros_like(acc)

    def body(q, carry):
        fetch(q).wait()
        live = live_ref[q]
        for t in range(slots):
            row = jnp.where(t < live, dst_ref[q, t], blocks)
            start = pl.multiple_of(src_ref[q, t] * blk, blk)
            acc[row] += jnp.dot(
                tile_vmem[q, t * blk : (t + 1) * blk, :],
                g_ref[q, pl.ds(start, blk), :],
                preferred_element_type=F32,
            )
        return carry

    lax.fori_loop(0, sources, body, 0)
    for d in range(blocks):
        half, rep = d % 2, d // 2
        out_ref[rep % 2, rep // 2, half * blk : (half + 1) * blk, :] = acc[d].astype(BF16)


def layer_kernel(
    dst_ref,
    src_ref,
    live_ref,
    part_ref,
    x_ref,
    ws_ref,
    wn_ref,
    bias_ref,
    deg_ref,
    cot_ref,
    tile_ref,
    out_ref,
    gin_ref,
    gs_ref,
    gn_ref,
    gb_ref,
    tile_vmem,
    core_in,
    chip_out,
    chip_in,
    gt,
    lhs,
    term,
    base,
    self_grad,
    ring_out,
    ring_in,
    col_out,
    col_in,
    wpart,
    win,
    rows_out,
    rows_in,
    rows_all,
    wfull,
    tile_sem,
    core_sem,
    chip_sem,
    gath_sem,
    fwd_sem,
    ring_sem,
    col_sem,
    w1_sem,
    w2_sem,
    w3_sem,
    w4_sem,
):
    loop = lax.axis_index("loop")
    rep = lax.axis_index("rep")
    core = rep % 2
    chip = rep // 2
    mate = (loop, chip * 2 + (1 - core))
    sources, depth, blk = tile_ref.shape
    slots = depth // blk
    blocks = gt.shape[0] - 1
    peers = 16

    barrier = pltpu.get_barrier_semaphore()

    def greet(j, carry):
        pl.semaphore_signal(
            barrier, inc=1, device_id=(loop, lax.rem(rep + j, peers)), device_id_type=MESH
        )
        pl.semaphore_signal(
            barrier, inc=1, device_id=(lax.rem(loop + j, peers), rep), device_id_type=MESH
        )
        return carry

    lax.fori_loop(1, peers, greet, 0)

    def fetch(q):
        return pltpu.make_async_copy(tile_ref.at[q], tile_vmem.at[q], tile_sem.at[q])

    for q in range(sources):
        fetch(q).start()
    base[...] = (
        jnp.dot(x_ref[...], ws_ref[...], preferred_element_type=F32) + bias_ref[...]
    )
    gt[blocks] = jnp.zeros(gt.shape[1:], BF16)
    pl.semaphore_wait(barrier, 2 * (peers - 1))

    steps = CHIP_STEPS + ((0, 0),)

    def core_copy(i):
        return remote(
            part_ref.at[1 - core, chip_node(*steps[i])],
            core_in.at[i],
            core_sem.at[0, i],
            core_sem.at[1, i],
            mate,
        )

    def chip_copy(i):
        return remote(
            chip_out.at[i],
            chip_in.at[i],
            chip_sem.at[0, i],
            chip_sem.at[1, i],
            (loop, chip_node(*steps[i]) * 2 + core),
        )

    for i in range(len(steps)):
        core_copy(i).start()
    for i in range(len(steps) - 1):
        core_copy(i).wait_recv()
        both = part_ref[core, chip_node(*steps[i])].astype(F32) + core_in[i].astype(F32)
        chip_out[i] = both.astype(BF16)
        if i > 0:
            chip_copy(i - 1).start()
    last = len(steps) - 1
    core_copy(last).wait_recv()
    total = part_ref[core, chip].astype(F32) + core_in[last].astype(F32)
    chip_copy(last - 1).start()
    for i in reversed(range(last)):
        chip_copy(i).wait_recv()
        total = total + chip_in[i].astype(F32)

    deg_rows = deg_ref[...].astype(F32)
    deg_cols = jnp.concatenate(
        [
            jnp.transpose(jnp.broadcast_to(deg_rows[s : s + 1, :], (blk, blk)))
            for s in range(2)
        ],
        axis=0,
    )
    aggregate = (total / deg_cols).astype(BF16)
    preact = base[...] + jnp.dot(aggregate, wn_ref[...], preferred_element_type=F32)
    sigmoid_val = jax.nn.sigmoid(preact)
    grad_pre = (
        cot_ref[...].astype(F32) * sigmoid_val * (1.0 + preact * (1.0 - sigmoid_val))
    ).astype(BF16)
    out_ref[...] = (preact * sigmoid_val).astype(BF16)
    back = lax.dot_general(
        wn_ref[...], grad_pre, (((1,), (1,)), ((), ())), preferred_element_type=F32
    )
    for s in range(2):
        gt[rep * 2 + s] = (back[:, s * blk : (s + 1) * blk] / deg_rows[s : s + 1, :]).astype(BF16)
    self_grad[...] = lax.dot_general(
        grad_pre, ws_ref[...], (((1,), (1,)), ((), ())), preferred_element_type=F32
    )

    def gather_copy(i):
        dy, dx = CHIP_STEPS[i]
        mine = gt.at[pl.ds(rep * 2, 2)]
        return remote(
            mine,
            mine,
            gath_sem.at[0, i],
            gath_sem.at[1, i],
            (loop, chip_node(dy, dx) * 2 + core),
        )

    def gathered(i):
        dy, dx = CHIP_STEPS[i]
        origin = chip_node((2 - dy) % 2, (X - dx) % X) * 2 + core
        return gt.at[pl.ds(origin * 2, 2)]

    def forward_copy(i):
        block = gathered(i) if i < len(CHIP_STEPS) else gt.at[pl.ds(rep * 2, 2)]
        return remote(block, block, fwd_sem.at[0, i], fwd_sem.at[1, i], mate)

    for i in range(len(CHIP_STEPS)):
        gather_copy(i).start()
    forward_copy(len(CHIP_STEPS)).start()

    wself = lax.dot_general(
        x_ref[...], grad_pre, (((0,), (0,)), ((), ())), preferred_element_type=F32
    )
    wneigh = lax.dot_general(
        aggregate, grad_pre, (((0,), (0,)), ((), ())), preferred_element_type=F32
    )
    wbias = jnp.sum(grad_pre.astype(F32), axis=0, keepdims=True)
    for j in range(8):
        wpart[j, 0:16, :] = wself[16 * j : 16 * j + 16, :]
        wpart[j + 8, 0:16, :] = wneigh[16 * j : 16 * j + 16, :]
        wpart[j, 16:24, :] = jnp.broadcast_to(wbias, (8, wbias.shape[1]))
        wpart[j + 8, 16:24, :] = jnp.broadcast_to(wbias, (8, wbias.shape[1]))

    def each_peer(action):
        def body(j, carry):
            action(j)
            return carry

        lax.fori_loop(1, peers, body, 0)

    def w1_copy(j, slot):
        to = lax.rem(rep + j, peers)
        return remote(
            wpart.at[to], win.at[slot], w1_sem.at[0, j], w1_sem.at[1, j], (loop, to)
        )

    def w2_copy(j, slot):
        to = lax.rem(loop + j, peers)
        return remote(
            rows_out.at[to], rows_in.at[slot], w2_sem.at[0, j], w2_sem.at[1, j], (to, rep)
        )

    def w3_copy(j, slot):
        to = lax.rem(loop + j, peers)
        return remote(
            rows_all.at[slot], rows_all.at[slot], w3_sem.at[0, j], w3_sem.at[1, j], (to, rep)
        )

    def w4_copy(j, slot):
        to = lax.rem(rep + j, peers)
        return remote(
            wfull.at[slot], wfull.at[slot], w4_sem.at[0, j], w4_sem.at[1, j], (loop, to)
        )

    each_peer(lambda j: w1_copy(j, rep).start())
    win[rep] = wpart[rep]

    for i in reversed(range(len(CHIP_STEPS))):
        block = gathered(i)
        remote(
            block, block, gath_sem.at[0, i], gath_sem.at[1, i], mate
        ).wait_recv()
        forward_copy(i).start()
    for i in range(len(CHIP_STEPS) + 1):
        if i < len(CHIP_STEPS):
            dy, dx = CHIP_STEPS[i]
            origin = chip_node((2 - dy) % 2, (X - dx) % X) * 2 + (1 - core)
        else:
            origin = chip * 2 + (1 - core)
        block = gt.at[pl.ds(origin * 2, 2)]
        remote(block, block, fwd_sem.at[0, i], fwd_sem.at[1, i], mate).wait_recv()
    for q in range(sources):
        fetch(q).wait()

    def compute(count, k):
        def body(j, carry):
            if k in (0, Z // 2):
                q = loop_node(k, 1 - j)
            else:
                q = loop_node(k * (1 - 2 * (j % 2)), 1 - j // 2)
            live = live_ref[q]
            for t in range(slots):
                d = dst_ref[q, t]
                s = src_ref[q, t]
                on = t < live
                lhs[0:blk, t * blk : (t + 1) * blk] = gt[
                    jnp.where(jnp.logical_and(on, s == 0), d, blocks)
                ]
                lhs[blk : 2 * blk, t * blk : (t + 1) * blk] = gt[
                    jnp.where(jnp.logical_and(on, s == 1), d, blocks)
                ]
            term[j] = jnp.dot(lhs[...], tile_vmem[q], preferred_element_type=F32)
            return carry

        lax.fori_loop(0, count, body, 0)

    def ring_copy(way, col, k):
        src = ring_out.at[way, col, k - 1]
        dst = ring_in.at[way, col, k - 1]
        if k == Z // 2:
            rows = pl.ds(way * blk, blk)
            src, dst = src.at[rows], dst.at[rows]
        return remote(
            src,
            dst,
            ring_sem.at[0, way, col, k - 1],
            ring_sem.at[1, way, col, k - 1],
            (loop_node(1 - 2 * way, 0), rep),
        )

    pending = []

    def launch(copy):
        if pending:
            pending.pop().start()
        if copy is not None:
            pending.append(copy)

    def ring_step(k):
        far = Z // 2
        compute(2 if k == far else 4, k)
        for col in (1, 0):
            for way in (0, 1):
                if k == far:
                    rows = slice(way * blk, (way + 1) * blk)
                    ring_out[way, col, k - 1, rows, :] = term[1 - col, rows, :].astype(BF16)
                else:
                    j = (1 - col) * 2 + way
                    ring_copy(way, col, k + 1).wait_recv()
                    if k == far - 1:
                        rows = slice(way * blk, (way + 1) * blk)
                        rest = slice((1 - way) * blk, (2 - way) * blk)
                        ring_out[way, col, k - 1, rows, :] = (
                            term[j, rows, :] + ring_in[way, col, k, rows, :].astype(F32)
                        ).astype(BF16)
                        ring_out[way, col, k - 1, rest, :] = term[j, rest, :].astype(BF16)
                    else:
                        ring_out[way, col, k - 1] = (
                            term[j] + ring_in[way, col, k].astype(F32)
                        ).astype(BF16)
                launch(ring_copy(way, col, k))
        launch(None)

    ring_step(4)

    each_peer(lambda j: w1_copy(j, lax.rem(rep + peers - j, peers)).wait_recv())
    piece = win[0]
    for j in range(1, peers):
        piece = piece + win[j]
    for m in range(peers):
        rows_out[m, 0:1, :] = piece[m : m + 1, :]
        rows_out[m, 1:2, :] = piece[16:17, :]
    each_peer(lambda j: w2_copy(j, loop).start())
    rows_in[loop] = rows_out[loop]

    ring_step(3)

    each_peer(lambda j: w2_copy(j, lax.rem(loop + peers - j, peers)).wait_recv())
    rows = rows_in[0]
    for j in range(1, peers):
        rows = rows + rows_in[j]
    rows_all[loop] = rows
    grad_scale = 1.0 / math.sqrt(x_ref.shape[0] * peers * peers)
    gb_ref[...] = rows[1:2, :] * grad_scale
    each_peer(lambda j: w3_copy(j, loop).start())

    ring_step(2)

    each_peer(lambda j: w3_copy(j, lax.rem(loop + peers - j, peers)).wait_recv())
    for m in range(peers):
        wfull[rep, m : m + 1, :] = rows_all[m, 0:1, :]
    each_peer(lambda j: w4_copy(j, rep).start())

    ring_step(1)

    compute(2, 0)
    for way in (0, 1):
        ring_copy(way, 1, 1).wait_recv()
    col_out[...] = (
        term[0] + ring_in[0, 1, 0].astype(F32) + ring_in[1, 1, 0].astype(F32)
    ).astype(BF16)
    each_peer(lambda j: w4_copy(j, lax.rem(rep + peers - j, peers)).wait_recv())
    col_copy = remote(col_out, col_in, col_sem.at[0], col_sem.at[1], (loop_node(0, 1), rep))
    col_copy.start()
    for j in range(8):
        gs_ref[16 * j : 16 * j + 16, :] = wfull[j] * grad_scale
        gn_ref[16 * j : 16 * j + 16, :] = wfull[j + 8] * grad_scale
    for way in (0, 1):
        ring_copy(way, 0, 1).wait_recv()
    mine = term[1] + ring_in[0, 0, 0].astype(F32) + ring_in[1, 0, 0].astype(F32)
    col_copy.wait_recv()
    mine = mine + col_in[...].astype(F32)
    for s in range(2):
        rows = slice(s * blk, (s + 1) * blk)
        gin_ref[rows, :] = (self_grad[rows, :] + jnp.transpose(mine[rows, :])).astype(BF16)

    for i in range(len(steps)):
        core_copy(i).wait_send()
        forward_copy(i).wait_send()
    for i in range(len(CHIP_STEPS)):
        chip_copy(i).wait_send()
        gather_copy(i).wait_send()
    for k in range(1, Z // 2 + 1):
        for col in (0, 1):
            for way in (0, 1):
                ring_copy(way, col, k).wait_send()
    col_copy.wait_send()
    each_peer(lambda j: w1_copy(j, rep).wait_send())
    each_peer(lambda j: w2_copy(j, loop).wait_send())
    each_peer(lambda j: w3_copy(j, loop).wait_send())
    each_peer(lambda j: w4_copy(j, rep).wait_send())


def per_device(
    features, w_self, w_neigh, bias, degree, tiles, dst_block, src_block, live_count, cotangent
):
    rows, feat = features.shape
    hidden = w_self.shape[1]
    sources, slots, blk = tiles.shape[2], tiles.shape[3], tiles.shape[4]
    tile_rows = tiles.reshape(sources, slots * blk, blk)
    dst = dst_block[0, 0]
    src = src_block[0, 0]
    live = live_count[0, 0]
    vmem = pl.BlockSpec(memory_space=pltpu.VMEM)
    smem = pl.BlockSpec(memory_space=pltpu.SMEM)
    hbm = pl.BlockSpec(memory_space=pl.ANY)
    dma = pltpu.SemaphoreType.DMA
    shape = jax.ShapeDtypeStruct

    gathered = pl.pallas_call(
        gather_kernel,
        out_shape=shape((sources, rows, feat), BF16),
        in_specs=[vmem],
        out_specs=vmem,
        scratch_shapes=[dma, dma((2,)), dma((2, 2, Z // 2)), dma((2, 2, Z // 2))],
        compiler_params=pltpu.CompilerParams(collective_id=0, has_side_effects=True),
        name="gather_features",
    )(features)

    blocks = 2 * 16
    partial = pl.pallas_call(
        product_kernel,
        out_shape=shape((2, 8, rows, feat), BF16),
        in_specs=[smem, smem, smem, vmem, hbm],
        out_specs=vmem,
        scratch_shapes=[
            pltpu.VMEM((sources, slots * blk, blk), BF16),
            pltpu.VMEM((blocks + 1, blk, feat), F32),
            dma((sources,)),
        ],
        compiler_params=pltpu.CompilerParams(vmem_limit_bytes=40 << 20),
        name="tile_product",
    )(dst, src, live, gathered, tile_rows)

    output, grad_input, grad_self, grad_neigh, grad_bias = pl.pallas_call(
        layer_kernel,
        out_shape=(
            shape((rows, hidden), BF16),
            shape((rows, feat), BF16),
            shape((feat, hidden), F32),
            shape((feat, hidden), F32),
            shape((1, hidden), F32),
        ),
        in_specs=[smem, smem, smem] + [vmem] * 7 + [hbm],
        out_specs=(vmem,) * 5,
        scratch_shapes=[
            pltpu.VMEM((sources, slots * blk, blk), BF16),
            pltpu.VMEM((8, rows, feat), BF16),
            pltpu.VMEM((7, rows, feat), BF16),
            pltpu.VMEM((7, rows, feat), BF16),
            pltpu.VMEM((blocks + 1, feat, blk), BF16),
            pltpu.VMEM((2 * feat, slots * blk), BF16),
            pltpu.VMEM((4, 2 * feat, blk), F32),
            pltpu.VMEM((rows, hidden), F32),
            pltpu.VMEM((rows, feat), F32),
            pltpu.VMEM((2, 2, Z // 2, 2 * feat, blk), BF16),
            pltpu.VMEM((2, 2, Z // 2, 2 * feat, blk), BF16),
            pltpu.VMEM((2 * feat, blk), BF16),
            pltpu.VMEM((2 * feat, blk), BF16),
            pltpu.VMEM((16, 24, hidden), F32),
            pltpu.VMEM((16, 24, hidden), F32),
            pltpu.VMEM((16, 2, hidden), F32),
            pltpu.VMEM((16, 2, hidden), F32),
            pltpu.VMEM((16, 2, hidden), F32),
            pltpu.VMEM((16, 16, hidden), F32),
            dma((sources,)),
            dma((2, 8)),
            dma((2, 7)),
            dma((2, 7)),
            dma((2, 8)),
            dma((2, 2, 2, Z // 2)),
            dma((2,)),
            dma((2, 16)),
            dma((2, 16)),
            dma((2, 16)),
            dma((2, 16)),
        ],
        compiler_params=pltpu.CompilerParams(
            collective_id=1, has_side_effects=True, vmem_limit_bytes=40 << 20
        ),
        name="layer",
    )(
        dst,
        src,
        live,
        partial,
        features,
        w_self,
        w_neigh,
        bias.reshape(1, hidden),
        degree.reshape(rows // blk, blk),
        cotangent,
        tile_rows,
    )
    return output, grad_input, grad_self, grad_neigh, grad_bias.reshape(hidden)


def solution(mesh):
    in_specs = (
        P(("loop", "rep"), None),
        P(),
        P(),
        P(),
        P(("loop", "rep")),
        P("loop", "rep", None, None, None, None),
        P("loop", "rep", None, None),
        P("loop", "rep", None, None),
        P("loop", "rep", None),
        P(("loop", "rep"), None),
    )
    out_specs = (P(("loop", "rep"), None), P(("loop", "rep"), None), P(), P(), P())
    return jax.shard_map(
        per_device, mesh=mesh, in_specs=in_specs, out_specs=out_specs, check_vma=False
    )
```

```python
import math

import jax
import jax.numpy as jnp
from jax import lax
from jax.experimental import pallas as pl
from jax.experimental.pallas import tpu as pltpu
from jax.sharding import PartitionSpec as P

F32 = jnp.float32
BF16 = jnp.bfloat16
MESH = pl.DeviceIdType.MESH
Z = 8
X = 4
CHIP_STEPS = ((1, 2), (1, 1), (1, 3), (0, 2), (1, 0), (0, 1), (0, 3))


def remote(src, dst, send_sem, recv_sem, device):
    return pltpu.make_async_remote_copy(
        src_ref=src,
        dst_ref=dst,
        send_sem=send_sem,
        recv_sem=recv_sem,
        device_id=device,
        device_id_type=MESH,
    )


def loop_node(dz, col):
    here = lax.axis_index("loop")
    z = lax.rem(here // 2 + (dz + Z), Z)
    return z * 2 + lax.rem(here % 2 + col, 2)


def chip_node(dy, dx):
    chip = lax.axis_index("rep") // 2
    return lax.rem(chip // X + dy, 2) * X + lax.rem(chip % X + dx, X)


FAR = Z // 2
STRIDE = {1: 1, 2: 2, 3: 1, 4: 2}


def layer_kernel(
    dst_hbm,
    src_hbm,
    live_hbm,
    x_hbm,
    ws_hbm,
    wn_hbm,
    bias_hbm,
    deg_hbm,
    cot_hbm,
    tile_hbm,
    out_ref,
    gin_ref,
    gs_ref,
    gn_ref,
    gb_ref,
    dst_ref,
    src_ref,
    live_ref,
    dst_v,
    live_v,
    x_ref,
    ws_ref,
    wn_ref,
    bias_ref,
    deg_ref,
    cot_ref,
    tile_ref,
    panels,
    here,
    prod,
    run,
    order_v,
    order,
    part,
    core_in,
    chip_out,
    chip_in,
    gt,
    term,
    base,
    self_grad,
    ring_out,
    ring_in,
    col_out,
    col_in,
    wpart,
    win,
    rows_in,
    wmate,
    wfull,
    tile_sem,
    load_sem,
    pair_sem,
    panel_sem,
    core_sem,
    chip_sem,
    gath_sem,
    fwd_sem,
    ring_sem,
    col_sem,
    w1_sem,
    w2_sem,
    w3_sem,
    second_sem,
    third_sem,
):
    loop = lax.axis_index("loop")
    rep = lax.axis_index("rep")
    core = rep % 2
    chip = rep // 2
    mate = (loop, chip * 2 + (1 - core))
    sources, depth, blk = tile_ref.shape
    slots = depth // blk
    total_slots = sources * slots
    blocks = gt.shape[0] - 1
    peers = 16
    left_chip, right_chip, over_chip = chip_node(0, X - 1), chip_node(0, 1), chip_node(1, 0)

    barrier = pltpu.get_barrier_semaphore()

    def greet(semaphore, device):
        pl.semaphore_signal(semaphore, inc=1, device_id=device, device_id_type=MESH)

    for dz, col in ((1, 0), (-1, 0), (2, 0), (-2, 0), (0, 1)):
        greet(barrier, (loop_node(dz, col), rep))
    for other in (left_chip, right_chip, over_chip):
        greet(barrier, (loop, other * 2 + core))
    greet(barrier, mate)

    loads = [
        pltpu.make_async_copy(a, b, load_sem.at[i])
        for i, (a, b) in enumerate(
            (
                (x_hbm, x_ref),
                (dst_hbm, dst_ref),
                (src_hbm, src_ref),
                (live_hbm, live_ref),
                (dst_hbm, dst_v),
                (live_hbm, live_v),
                (ws_hbm, ws_ref),
                (wn_hbm, wn_ref),
                (bias_hbm, bias_ref),
                (deg_hbm, deg_ref),
                (cot_hbm, cot_ref),
            )
        )
    ]
    for copy in loads:
        copy.start()

    def fetch(q):
        return pltpu.make_async_copy(tile_hbm.at[q], tile_ref.at[q], tile_sem.at[q])

    near_first = [(0, 0), (0, 1)]
    for k in range(1, FAR):
        near_first += [(k, 0), (-k, 0), (k, 1), (-k, 1)]
    near_first += [(FAR, 0), (FAR, 1)]
    for dz, col in near_first:
        fetch(loop_node(dz, col)).start()
    loads[0].wait()
    pl.semaphore_wait(barrier, 9)
    def panel(origin, k, s):
        if k == 0:
            return x_ref.at[pl.ds(s * blk, blk)]
        return panels.at[origin * 2 + s]

    def hop(way, col, k, s):
        sign = 1 - 2 * way
        origin = loop_node(0 if k < 3 else -2 * sign, col)
        return remote(
            panel(origin, col if k < 3 else 2, s),
            panels.at[origin * 2 + s],
            panel_sem.at[0, way, col, k - 1, s],
            panel_sem.at[1, way, col, k - 1, s],
            (loop_node(sign * STRIDE[k], 0), rep),
        )

    def arrival(way, col, k, s):
        sign = 1 - 2 * way
        dst = panels.at[loop_node(-sign * k, col) * 2 + s]
        return remote(
            dst,
            dst,
            panel_sem.at[0, way, col, k - 1, s],
            panel_sem.at[1, way, col, k - 1, s],
            (loop_node(sign, 0), rep),
        )

    def pair(s, col):
        rows = pl.ds(s * blk, blk)
        return remote(
            x_ref.at[rows],
            panels.at[loop_node(0, col) * 2 + s],
            pair_sem.at[0, s],
            pair_sem.at[1, s],
            (loop_node(0, 1), rep),
        )

    def on_route(way, k, s):
        return k < FAR or s == way

    for s in range(2):
        pair(s, 0).start()
        for way in (0, 1):
            hop(way, 0, 2, s).start()
    for s in range(2):
        for way in (0, 1):
            hop(way, 0, 1, s).start()
    for other in (left_chip, right_chip):
        greet(second_sem, (loop, other * 2 + core))
    for copy in loads[1:]:
        copy.wait()
    for s in range(2):
        panels[loop * 2 + s] = x_ref[s * blk : (s + 1) * blk, :]
    gt[blocks] = jnp.zeros(gt.shape[1:], BF16)
    run[total_slots] = jnp.zeros(run.shape[1:], BF16)

    def multiply(q):
        fetch(q).wait()
        for s in range(2):
            here[s] = panels[q * 2 + s]
        for t in range(slots):
            prod[q * slots + t] = jnp.dot(
                tile_ref[q, t * blk : (t + 1) * blk, :],
                here[src_ref[q, t]],
                preferred_element_type=F32,
            )

    def multiply_some(nodes):
        count = len(nodes)

        def body(j, carry):
            q = nodes[-1]
            for i in range(count - 1):
                q = jnp.where(j == i, nodes[i], q)
            multiply(q)
            return carry

        lax.fori_loop(0, count, body, 0)

    def sort_slots():
        slot_col = lax.broadcasted_iota(jnp.int32, (sources, slots), 1)
        live_eye = lax.broadcasted_iota(jnp.int32, (sources, sources), 0) == (
            lax.broadcasted_iota(jnp.int32, (sources, sources), 1)
        )
        live_rows = jnp.sum(
            jnp.where(live_eye, jnp.broadcast_to(live_v[...], (sources, sources)), 0),
            axis=1,
            keepdims=True,
        )
        key_grid = jnp.where(slot_col < live_rows, dst_v[...], blocks)
        spread = (
            lax.broadcasted_iota(jnp.int32, (slots, total_slots), 1) % slots
            == lax.broadcasted_iota(jnp.int32, (slots, total_slots), 0)
        )
        pick = (
            lax.broadcasted_iota(jnp.int32, (sources, total_slots), 1) // slots
            == lax.broadcasted_iota(jnp.int32, (sources, total_slots), 0)
        )
        wide = jnp.dot(
            key_grid.astype(F32).astype(BF16),
            spread.astype(F32).astype(BF16),
            preferred_element_type=F32,
        )
        key_row = jnp.sum(jnp.where(pick, wide, 0.0), axis=0, keepdims=True).astype(jnp.int32)
        square = (total_slots, total_slots)
        down = lax.broadcasted_iota(jnp.int32, square, 0)
        across = lax.broadcasted_iota(jnp.int32, square, 1)
        keys = jnp.broadcast_to(key_row, square)
        key_col = jnp.sum(jnp.where(down == across, keys, 0), axis=1, keepdims=True)
        before = jnp.logical_or(
            keys < key_col, jnp.logical_and(keys == key_col, across < down)
        )
        rank = jnp.sum(before.astype(jnp.int32), axis=1, keepdims=True)
        placed = rank == across
        order_v[0:1, :] = jnp.sum(jnp.where(placed, down, 0), axis=0, keepdims=True)
        order_v[1:2, :] = jnp.sum(jnp.where(placed, key_col, 0), axis=0, keepdims=True)
        order_v[2:3, :] = jnp.sum((key_col <= across).astype(jnp.int32), axis=0, keepdims=True)
        order_v[3:4, :] = jnp.sum((key_col == across).astype(jnp.int32), axis=0, keepdims=True)
        order_v[4:8, :] = jnp.zeros((4, total_slots), jnp.int32)
        order_copy().start()

    def order_copy():
        return pltpu.make_async_copy(order_v, order, load_sem.at[11])

    def relay(col):
        for s in range(2):
            for way in (0, 1):
                arrival(way, col, 2, s).wait_recv()
                hop(way, col, 3, s).start()
                if s == way:
                    hop(way, col, 4, s).start()

    def take(k, col):
        for s in range(2):
            for way in (0, 1):
                if on_route(way, k, s):
                    arrival(way, col, k, s).wait_recv()

    def multiply_at(k, col):
        if k in (0, FAR):
            multiply_some([loop_node(k, col)])
        else:
            multiply_some([loop_node(k, col), loop_node(-k, col)])

    multiply_at(0, 0)
    for s in range(2):
        pair(s, 1).wait_recv()
        for way in (0, 1):
            hop(way, 1, 2, s).start()
    for s in range(2):
        for way in (0, 1):
            hop(way, 1, 1, s).start()
    multiply_at(0, 1)
    relay(0)
    take(1, 0)
    multiply_at(1, 0)
    relay(1)
    take(1, 1)
    multiply_at(1, 1)
    base[...] = (
        jnp.dot(x_ref[...], ws_ref[...], preferred_element_type=F32) + bias_ref[...]
    )
    sort_slots()
    pl.semaphore_wait(second_sem, 2)
    for other in (left_chip, right_chip):
        greet(third_sem, (loop, other * 2 + core))
    for col in (0, 1):
        multiply_at(2, col)
    for col in (0, 1):
        take(3, col)
        multiply_at(3, col)
        take(4, col)
        multiply_at(4, col)
    order_copy().wait()
    pl.semaphore_wait(third_sem, 2)

    def accumulate(i, total):
        for u in range(8):
            j = i * 8 + u
            same = jnp.logical_and(j > 0, order[1, j] == order[1, jnp.maximum(j - 1, 0)])
            total = total * jnp.where(same, 1.0, 0.0) + prod[order[0, j]]
            run[j] = total.astype(BF16)
        return total

    lax.fori_loop(0, total_slots // 8, accumulate, jnp.zeros((blk, blk), F32))

    steps = CHIP_STEPS + ((0, 0),)

    def collect(side, i):
        for s in range(2):
            which = core if side == 0 else 1 - core
            d = (chip_node(*steps[i]) * 2 + which) * 2 + s
            part[side, i, s * blk : (s + 1) * blk, :] = run[
                jnp.where(order[3, d] > 0, order[2, d] - 1, total_slots)
            ]

    def core_copy(i):
        return remote(
            part.at[1, i], core_in.at[i], core_sem.at[0, i], core_sem.at[1, i], mate
        )

    def chip_copy(i):
        return remote(
            chip_out.at[i],
            chip_in.at[i],
            chip_sem.at[0, i],
            chip_sem.at[1, i],
            (loop, chip_node(*steps[i]) * 2 + core),
        )

    for i in range(len(steps)):
        collect(1, i)
        if i > 0:
            core_copy(i - 1).start()
    last = len(steps) - 1
    collect(0, 0)
    core_copy(last).start()
    for i in range(last):
        collect(0, i + 1)
        core_copy(i).wait_recv()
        both = part[0, i].astype(F32) + core_in[i].astype(F32)
        chip_out[i] = both.astype(BF16)
        if i > 0:
            chip_copy(i - 1).start()
    core_copy(last).wait_recv()
    total = part[0, last].astype(F32) + core_in[last].astype(F32)
    chip_copy(last - 1).start()
    for i in reversed(range(last)):
        chip_copy(i).wait_recv()
        total = total + chip_in[i].astype(F32)

    deg_rows = deg_ref[...].astype(F32)
    deg_cols = jnp.concatenate(
        [
            jnp.transpose(jnp.broadcast_to(deg_rows[s : s + 1, :], (blk, blk)))
            for s in range(2)
        ],
        axis=0,
    )
    aggregate = (total / deg_cols).astype(BF16)
    preact = base[...] + jnp.dot(aggregate, wn_ref[...], preferred_element_type=F32)
    sigmoid_val = jax.nn.sigmoid(preact)
    grad_pre = (
        cot_ref[...].astype(F32) * sigmoid_val * (1.0 + preact * (1.0 - sigmoid_val))
    ).astype(BF16)
    out_ref[...] = (preact * sigmoid_val).astype(BF16)
    back = lax.dot_general(
        wn_ref[...], grad_pre, (((1,), (1,)), ((), ())), preferred_element_type=F32
    )
    for s in range(2):
        gt[rep * 2 + s] = (back[:, s * blk : (s + 1) * blk] / deg_rows[s : s + 1, :]).astype(BF16)
    self_grad[...] = lax.dot_general(
        grad_pre, ws_ref[...], (((1,), (1,)), ((), ())), preferred_element_type=F32
    )

    def gather_copy(i):
        dy, dx = CHIP_STEPS[i]
        mine = gt.at[pl.ds(rep * 2, 2)]
        return remote(
            mine,
            mine,
            gath_sem.at[0, i],
            gath_sem.at[1, i],
            (loop, chip_node(dy, dx) * 2 + core),
        )

    def gathered(i):
        dy, dx = CHIP_STEPS[i]
        origin = chip_node((2 - dy) % 2, (X - dx) % X) * 2 + core
        return gt.at[pl.ds(origin * 2, 2)]

    def forward_copy(i):
        block = gathered(i) if i < len(CHIP_STEPS) else gt.at[pl.ds(rep * 2, 2)]
        return remote(block, block, fwd_sem.at[0, i], fwd_sem.at[1, i], mate)

    for i in range(len(CHIP_STEPS)):
        gather_copy(i).start()
    forward_copy(len(CHIP_STEPS)).start()

    wself = lax.dot_general(
        x_ref[...], grad_pre, (((0,), (0,)), ((), ())), preferred_element_type=F32
    )
    wneigh = lax.dot_general(
        aggregate, grad_pre, (((0,), (0,)), ((), ())), preferred_element_type=F32
    )
    wbias = jnp.sum(grad_pre.astype(F32), axis=0, keepdims=True)
    for j in range(8):
        wpart[j, 0:16, :] = wself[16 * j : 16 * j + 16, :]
        wpart[j + 8, 0:16, :] = wneigh[16 * j : 16 * j + 16, :]
        wpart[j, 16:24, :] = jnp.broadcast_to(wbias, (8, wbias.shape[1]))
        wpart[j + 8, 16:24, :] = jnp.broadcast_to(wbias, (8, wbias.shape[1]))
    piece = core * 8 + chip

    def w1_mate():
        return remote(
            wpart.at[pl.ds((1 - core) * 8, 8)], wmate, w1_sem.at[0, 7], w1_sem.at[1, 7], mate
        )

    def w1_copy(i, sending):
        dy, dx = CHIP_STEPS[i]
        slot = chip if sending else chip_node((2 - dy) % 2, (X - dx) % X)
        to = chip_node(dy, dx)
        return remote(
            wpart.at[core * 8 + to],
            win.at[slot],
            w1_sem.at[0, i],
            w1_sem.at[1, i],
            (loop, to * 2 + core),
        )

    def w2_copy(stage, j, sending):
        step = 4**stage
        own = loop // step % 4
        to = loop + (lax.rem(own + j, 4) - own) * step
        slot = own if sending else lax.rem(own + 4 - j, 4)
        block = rows_in.at[stage, slot]
        return remote(
            block, block, w2_sem.at[0, stage, j], w2_sem.at[1, stage, j], (to, rep)
        )

    def w2_send(stage, value):
        rows_in[stage, loop // 4**stage % 4] = value
        for j in range(1, 4):
            pending.append(w2_copy(stage, j, True))

    def w2_sum(stage):
        for j in range(1, 4):
            w2_copy(stage, j, False).wait_recv()
        value = rows_in[stage, 0]
        for j in range(1, 4):
            value = value + rows_in[stage, j]
        return value

    def w3_copy(i, sending):
        dy, dx = CHIP_STEPS[i]
        slot = chip if sending else chip_node((2 - dy) % 2, (X - dx) % X)
        block = wfull.at[core * 8 + slot]
        return remote(
            block,
            block,
            w3_sem.at[0, i],
            w3_sem.at[1, i],
            (loop, chip_node(dy, dx) * 2 + core),
        )

    def w3_mate(side):
        block = wfull.at[pl.ds(side * 8, 8)]
        return remote(block, block, w3_sem.at[0, 7], w3_sem.at[1, 7], mate)

    w1_mate().start()
    for i in reversed(range(len(CHIP_STEPS))):
        block = gathered(i)
        remote(
            block, block, gath_sem.at[0, i], gath_sem.at[1, i], mate
        ).wait_recv()
        forward_copy(i).start()
        if i == 4:
            w1_mate().wait_recv()
            for j in range(8):
                wpart[core * 8 + j] = wpart[core * 8 + j] + wmate[j]
            win[chip] = wpart[piece]
        if i == 3:
            for j in range(len(CHIP_STEPS)):
                w1_copy(j, True).start()
    for i in range(len(CHIP_STEPS) + 1):
        if i < len(CHIP_STEPS):
            dy, dx = CHIP_STEPS[i]
            origin = chip_node((2 - dy) % 2, (X - dx) % X) * 2 + (1 - core)
        else:
            origin = chip * 2 + (1 - core)
        block = gt.at[pl.ds(origin * 2, 2)]
        remote(block, block, fwd_sem.at[0, i], fwd_sem.at[1, i], mate).wait_recv()

    def compute(count, k, first):
        def body(j, carry):
            if k in (0, FAR):
                q = loop_node(k, 1 - j)
            else:
                q = loop_node(k * (1 - 2 * (j % 2)), 1 - j // 2)
            sums = [jnp.zeros((blk, blk), F32) for _ in range(2)]
            for t in range(slots):
                d = jnp.where(t < live_ref[0, q], dst_ref[q, t], blocks)
                value = jnp.dot(
                    gt[d], tile_ref[q, t * blk : (t + 1) * blk, :], preferred_element_type=F32
                )
                for s in range(2):
                    sums[s] = sums[s] + value * jnp.where(src_ref[q, t] == s, 1.0, 0.0)
            for s in range(2):
                term[first + j, s * blk : (s + 1) * blk, :] = sums[s]
            return carry

        lax.fori_loop(0, count, body, 0)

    def ring_copy(way, col, k, s):
        rows = pl.ds(s * blk, blk)
        return remote(
            ring_out.at[way, col, k - 1, rows],
            ring_in.at[way, col, k - 1, rows],
            ring_sem.at[0, way, col, k - 1, s],
            ring_sem.at[1, way, col, k - 1, s],
            (loop_node((1 - 2 * way) * STRIDE[k], 0), rep),
        )

    pending = []

    def launch(copy):
        while pending:
            pending.pop(0).start()
        if copy is not None:
            pending.append(copy)

    def ring_send(k, first, cols):
        for col in cols:
            for s in range(2):
                rows = slice(s * blk, (s + 1) * blk)
                for way in (0, 1):
                    if not on_route(way, k, s):
                        continue
                    j = first + (1 - col if k == FAR else (1 - col) * 2 + way)
                    value = term[j, rows, :]
                    if k == 2:
                        ring_copy(way, col, 3, s).wait_recv()
                        value = value + ring_in[way, col, 2, rows, :].astype(F32)
                        if s == way:
                            ring_copy(way, col, 4, s).wait_recv()
                            value = value + ring_in[way, col, 3, rows, :].astype(F32)
                    ring_out[way, col, k - 1, rows, :] = value.astype(BF16)
                    launch(ring_copy(way, col, k, s))

    compute(4, 3, 0)
    ring_send(3, 0, (1, 0))
    compute(2, FAR, 4)
    ring_send(FAR, 4, (1, 0))
    launch(None)
    compute(4, 2, 0)
    for i in reversed(range(len(CHIP_STEPS))):
        w1_copy(i, False).wait_recv()
    value = win[0]
    for j in range(1, 8):
        value = value + win[j]
    w2_send(0, value)
    compute(4, 1, 4)
    ring_send(1, 4, (1, 0))
    ring_send(2, 0, (1,))
    w2_send(1, w2_sum(0))
    ring_send(2, 0, (0,))
    launch(None)
    compute(2, 0, 0)
    grad_scale = 1.0 / math.sqrt(x_ref.shape[0] * peers * peers)
    value = w2_sum(1)
    gb_ref[...] = value[16:17, :] * grad_scale
    wfull[piece] = value[0:16, :] * grad_scale

    def arrived(col, s):
        rows = slice(s * blk, (s + 1) * blk)
        value = term[1 - col, rows, :]
        for way in (0, 1):
            for k in (1, 2):
                ring_copy(way, col, k, s).wait_recv()
                value = value + ring_in[way, col, k - 1, rows, :].astype(F32)
        return value

    def col_copy(s):
        rows = pl.ds(s * blk, blk)
        return remote(
            col_out.at[rows],
            col_in.at[rows],
            col_sem.at[0, s],
            col_sem.at[1, s],
            (loop_node(0, 1), rep),
        )

    for s in range(2):
        col_out[s * blk : (s + 1) * blk, :] = arrived(1, s).astype(BF16)
        if s == 0:
            for i in range(len(CHIP_STEPS)):
                w3_copy(i, True).start()
        else:
            col_copy(0).start()
    mine = [arrived(0, 0)]
    col_copy(1).start()
    mine.append(arrived(0, 1))
    for i in reversed(range(len(CHIP_STEPS))):
        w3_copy(i, False).wait_recv()
    w3_mate(core).start()
    for s in range(2):
        rows = slice(s * blk, (s + 1) * blk)
        col_copy(s).wait_recv()
        value = mine[s] + col_in[rows, :].astype(F32)
        gin_ref[rows, :] = (self_grad[rows, :] + jnp.transpose(value)).astype(BF16)
    w3_mate(1 - core).wait_recv()
    for j in range(8):
        gs_ref[16 * j : 16 * j + 16, :] = wfull[j]
        gn_ref[16 * j : 16 * j + 16, :] = wfull[j + 8]

    for s in range(2):
        pair(s, 0).wait_send()
        col_copy(s).wait_send()
    for i in range(len(steps)):
        core_copy(i).wait_send()
        forward_copy(i).wait_send()
    for i in range(len(CHIP_STEPS)):
        chip_copy(i).wait_send()
        gather_copy(i).wait_send()
    for k in range(1, FAR + 1):
        for col in (0, 1):
            for s in range(2):
                for way in (0, 1):
                    if on_route(way, k, s):
                        hop(way, col, k, s).wait_send()
                        ring_copy(way, col, k, s).wait_send()
    for i in range(len(CHIP_STEPS)):
        w1_copy(i, True).wait_send()
        w3_copy(i, True).wait_send()
    for stage in range(2):
        for j in range(1, 4):
            w2_copy(stage, j, True).wait_send()
    w1_mate().wait_send()
    w3_mate(core).wait_send()


def finish_kernel(*refs):
    for a, b in zip(refs[:5], refs[5:]):
        b[...] = a[...]


def per_device(
    features, w_self, w_neigh, bias, degree, tiles, dst_block, src_block, live_count, cotangent
):
    rows, feat = features.shape
    hidden = w_self.shape[1]
    sources, slots, blk = tiles.shape[2], tiles.shape[3], tiles.shape[4]
    blocks = 2 * 16
    vmem = pl.BlockSpec(memory_space=pltpu.VMEM)
    hbm = pl.BlockSpec(memory_space=pl.ANY)
    dma = pltpu.SemaphoreType.DMA
    shape = jax.ShapeDtypeStruct
    smem = pltpu.SMEM

    results = (
        shape((rows, hidden), BF16),
        shape((rows, feat), BF16),
        shape((feat, hidden), F32),
        shape((feat, hidden), F32),
        shape((1, hidden), F32),
    )
    made = pl.pallas_call(
        layer_kernel,
        out_shape=results,
        in_specs=[hbm] * 10,
        out_specs=(vmem,) * 5,
        scratch_shapes=[
            smem((sources, slots), jnp.int32),
            smem((sources, slots), jnp.int32),
            smem((1, sources), jnp.int32),
            pltpu.VMEM((sources, slots), jnp.int32),
            pltpu.VMEM((1, sources), jnp.int32),
            pltpu.VMEM((rows, feat), BF16),
            pltpu.VMEM((feat, hidden), BF16),
            pltpu.VMEM((feat, hidden), BF16),
            pltpu.VMEM((1, hidden), F32),
            pltpu.VMEM((rows // blk, blk), jnp.int32),
            pltpu.VMEM((rows, hidden), BF16),
            pltpu.VMEM((sources, slots * blk, blk), BF16),
            pltpu.VMEM((sources * 2, blk, feat), BF16),
            pltpu.VMEM((2, blk, feat), BF16),
            pltpu.VMEM((sources * slots, blk, feat), F32),
            pltpu.VMEM((sources * slots + 1, blk, feat), BF16),
            pltpu.VMEM((8, sources * slots), jnp.int32),
            smem((8, sources * slots), jnp.int32),
            pltpu.VMEM((2, 8, rows, feat), BF16),
            pltpu.VMEM((8, rows, feat), BF16),
            pltpu.VMEM((7, rows, feat), BF16),
            pltpu.VMEM((7, rows, feat), BF16),
            pltpu.VMEM((blocks + 1, feat, blk), BF16),
            pltpu.VMEM((8, 2 * feat, blk), F32),
            pltpu.VMEM((rows, hidden), F32),
            pltpu.VMEM((rows, feat), F32),
            pltpu.VMEM((2, 2, FAR, 2 * feat, blk), BF16),
            pltpu.VMEM((2, 2, FAR, 2 * feat, blk), BF16),
            pltpu.VMEM((2 * feat, blk), BF16),
            pltpu.VMEM((2 * feat, blk), BF16),
            pltpu.VMEM((16, 24, hidden), F32),
            pltpu.VMEM((8, 24, hidden), F32),
            pltpu.VMEM((2, 4, 24, hidden), F32),
            pltpu.VMEM((8, 24, hidden), F32),
            pltpu.VMEM((16, 16, hidden), F32),
            dma((sources,)),
            dma((12,)),
            dma((2, 2)),
            dma((2, 2, 2, FAR, 2)),
            dma((2, 8)),
            dma((2, 7)),
            dma((2, 7)),
            dma((2, 8)),
            dma((2, 2, 2, FAR, 2)),
            dma((2, 2)),
            dma((2, 8)),
            dma((2, 2, 4)),
            dma((2, 8)),
            pltpu.SemaphoreType.REGULAR,
            pltpu.SemaphoreType.REGULAR,
        ],
        compiler_params=pltpu.CompilerParams(
            collective_id=0, has_side_effects=True, vmem_limit_bytes=57 << 20
        ),
        name="layer",
    )(
        dst_block.reshape(sources, slots),
        src_block.reshape(sources, slots),
        live_count.reshape(1, sources),
        features,
        w_self,
        w_neigh,
        bias.reshape(1, hidden),
        degree.reshape(rows // blk, blk),
        cotangent,
        tiles.reshape(sources, slots * blk, blk),
    )
    output, grad_input, grad_self, grad_neigh, grad_bias = pl.pallas_call(
        finish_kernel,
        out_shape=results,
        in_specs=[vmem] * 5,
        out_specs=(vmem,) * 5,
        name="finish",
    )(*made)
    return output, grad_input, grad_self, grad_neigh, grad_bias.reshape(hidden)


def solution(mesh):
    in_specs = (
        P(("loop", "rep"), None),
        P(),
        P(),
        P(),
        P(("loop", "rep")),
        P("loop", "rep", None, None, None, None),
        P("loop", "rep", None, None),
        P("loop", "rep", None, None),
        P("loop", "rep", None),
        P(("loop", "rep"), None),
    )
    out_specs = (P(("loop", "rep"), None), P(("loop", "rep"), None), P(), P(), P())
    return jax.shard_map(
        per_device, mesh=mesh, in_specs=in_specs, out_specs=out_specs, check_vma=False
    )
```

```python
import math

import jax
import jax.numpy as jnp
from jax import lax
from jax.experimental import pallas as pl
from jax.experimental.pallas import tpu as pltpu
from jax.sharding import PartitionSpec as P

F32 = jnp.float32
BF16 = jnp.bfloat16
MESH = pl.DeviceIdType.MESH
Z = 8
X = 4
CHIP_STEPS = ((1, 2), (1, 1), (1, 3), (0, 2), (1, 0), (0, 1), (0, 3))


def remote(src, dst, send_sem, recv_sem, device):
    return pltpu.make_async_remote_copy(
        src_ref=src,
        dst_ref=dst,
        send_sem=send_sem,
        recv_sem=recv_sem,
        device_id=device,
        device_id_type=MESH,
    )


def loop_node(dz, col):
    here = lax.axis_index("loop")
    z = lax.rem(here // 2 + (dz + Z), Z)
    return z * 2 + lax.rem(here % 2 + col, 2)


def chip_node(dy, dx):
    chip = lax.axis_index("rep") // 2
    return lax.rem(chip // X + dy, 2) * X + lax.rem(chip % X + dx, X)


FAR = Z // 2
STRIDE = {1: 1, 2: 2, 3: 1, 4: 2}


def layer_kernel(
    dst_hbm,
    src_hbm,
    live_hbm,
    x_hbm,
    ws_hbm,
    wn_hbm,
    bias_hbm,
    deg_hbm,
    cot_hbm,
    tile_hbm,
    out_ref,
    gin_ref,
    gs_ref,
    gn_ref,
    gb_ref,
    dst_ref,
    src_ref,
    live_ref,
    dst_v,
    live_v,
    x_ref,
    ws_ref,
    wn_ref,
    bias_ref,
    deg_ref,
    cot_ref,
    tile_ref,
    panels,
    here,
    prod,
    run,
    order_v,
    order,
    part,
    core_in,
    chip_out,
    chip_in,
    gt,
    term,
    base,
    self_grad,
    ring_out,
    ring_in,
    col_out,
    col_in,
    wpart,
    win,
    rows_in,
    wmate,
    wfull,
    tile_sem,
    load_sem,
    pair_sem,
    panel_sem,
    core_sem,
    chip_sem,
    gath_sem,
    fwd_sem,
    ring_sem,
    col_sem,
    w1_sem,
    w2_sem,
    w3_sem,
    second_sem,
    third_sem,
):
    loop = lax.axis_index("loop")
    rep = lax.axis_index("rep")
    core = rep % 2
    chip = rep // 2
    mate = (loop, chip * 2 + (1 - core))
    sources, depth, blk = tile_ref.shape
    slots = depth // blk
    total_slots = sources * slots
    blocks = gt.shape[0] - 1
    peers = 16
    left_chip, right_chip, over_chip = chip_node(0, X - 1), chip_node(0, 1), chip_node(1, 0)

    barrier = pltpu.get_barrier_semaphore()

    def greet(semaphore, device):
        pl.semaphore_signal(semaphore, inc=1, device_id=device, device_id_type=MESH)

    for dz, col in ((1, 0), (-1, 0), (2, 0), (-2, 0), (0, 1)):
        greet(barrier, (loop_node(dz, col), rep))
    for other in (left_chip, right_chip, over_chip):
        greet(barrier, (loop, other * 2 + core))
    greet(barrier, mate)

    loads = [
        pltpu.make_async_copy(a, b, load_sem.at[i])
        for i, (a, b) in enumerate(
            (
                (x_hbm, x_ref),
                (dst_hbm, dst_ref),
                (src_hbm, src_ref),
                (live_hbm, live_ref),
                (dst_hbm, dst_v),
                (live_hbm, live_v),
                (ws_hbm, ws_ref),
                (wn_hbm, wn_ref),
                (bias_hbm, bias_ref),
                (deg_hbm, deg_ref),
                (cot_hbm, cot_ref),
            )
        )
    ]
    for copy in loads:
        copy.start()

    def fetch(q):
        return pltpu.make_async_copy(tile_hbm.at[q], tile_ref.at[q], tile_sem.at[q])

    near_first = [(0, 0), (0, 1)]
    for k in range(1, FAR):
        near_first += [(k, 0), (-k, 0), (k, 1), (-k, 1)]
    near_first += [(FAR, 0), (FAR, 1)]
    for dz, col in near_first:
        fetch(loop_node(dz, col)).start()
    loads[0].wait()
    pl.semaphore_wait(barrier, 9)
    def panel(origin, k, s):
        if k == 0:
            return x_ref.at[pl.ds(s * blk, blk)]
        return panels.at[origin * 2 + s]

    def hop(way, col, k, s):
        sign = 1 - 2 * way
        if col == 1 and k > 1:
            block = panels.at[loop_node(-sign * k, 0) * 2 + s]
            return remote(
                block,
                block,
                panel_sem.at[0, way, col, k - 1, s],
                panel_sem.at[1, way, col, k - 1, s],
                (loop_node(0, 1), rep),
            )
        origin = loop_node(0 if k < 3 else -2 * sign, col)
        return remote(
            panel(origin, col if k < 3 else 2, s),
            panels.at[origin * 2 + s],
            panel_sem.at[0, way, col, k - 1, s],
            panel_sem.at[1, way, col, k - 1, s],
            (loop_node(sign * STRIDE[k], 0), rep),
        )

    def arrival(way, col, k, s):
        sign = 1 - 2 * way
        dst = panels.at[loop_node(-sign * k, col) * 2 + s]
        return remote(
            dst,
            dst,
            panel_sem.at[0, way, col, k - 1, s],
            panel_sem.at[1, way, col, k - 1, s],
            (loop_node(sign, 0), rep),
        )

    def pair(s, col):
        rows = pl.ds(s * blk, blk)
        return remote(
            x_ref.at[rows],
            panels.at[loop_node(0, col) * 2 + s],
            pair_sem.at[0, s],
            pair_sem.at[1, s],
            (loop_node(0, 1), rep),
        )

    def on_route(way, k, s):
        return k < FAR or s == way

    for s in range(2):
        pair(s, 0).start()
        for way in (0, 1):
            hop(way, 0, 2, s).start()
    for s in range(2):
        for way in (0, 1):
            hop(way, 0, 1, s).start()
    for other in (left_chip, right_chip):
        greet(second_sem, (loop, other * 2 + core))
    for copy in loads[1:]:
        copy.wait()
    for s in range(2):
        panels[loop * 2 + s] = x_ref[s * blk : (s + 1) * blk, :]
    gt[blocks] = jnp.zeros(gt.shape[1:], BF16)
    run[total_slots] = jnp.zeros(run.shape[1:], BF16)

    def multiply(q):
        fetch(q).wait()
        for s in range(2):
            here[s] = panels[q * 2 + s]
        for t in range(slots):
            prod[q * slots + t] = jnp.dot(
                tile_ref[q, t * blk : (t + 1) * blk, :],
                here[src_ref[q, t]],
                preferred_element_type=F32,
            )

    def multiply_some(nodes):
        count = len(nodes)

        def body(j, carry):
            q = nodes[-1]
            for i in range(count - 1):
                q = jnp.where(j == i, nodes[i], q)
            multiply(q)
            return carry

        lax.fori_loop(0, count, body, 0)

    def sort_slots():
        slot_col = lax.broadcasted_iota(jnp.int32, (sources, slots), 1)
        live_eye = lax.broadcasted_iota(jnp.int32, (sources, sources), 0) == (
            lax.broadcasted_iota(jnp.int32, (sources, sources), 1)
        )
        live_rows = jnp.sum(
            jnp.where(live_eye, jnp.broadcast_to(live_v[...], (sources, sources)), 0),
            axis=1,
            keepdims=True,
        )
        key_grid = jnp.where(slot_col < live_rows, dst_v[...], blocks)
        spread = (
            lax.broadcasted_iota(jnp.int32, (slots, total_slots), 1) % slots
            == lax.broadcasted_iota(jnp.int32, (slots, total_slots), 0)
        )
        pick = (
            lax.broadcasted_iota(jnp.int32, (sources, total_slots), 1) // slots
            == lax.broadcasted_iota(jnp.int32, (sources, total_slots), 0)
        )
        wide = jnp.dot(
            key_grid.astype(F32).astype(BF16),
            spread.astype(F32).astype(BF16),
            preferred_element_type=F32,
        )
        key_row = jnp.sum(jnp.where(pick, wide, 0.0), axis=0, keepdims=True).astype(jnp.int32)
        square = (total_slots, total_slots)
        down = lax.broadcasted_iota(jnp.int32, square, 0)
        across = lax.broadcasted_iota(jnp.int32, square, 1)
        keys = jnp.broadcast_to(key_row, square)
        key_col = jnp.sum(jnp.where(down == across, keys, 0), axis=1, keepdims=True)
        before = jnp.logical_or(
            keys < key_col, jnp.logical_and(keys == key_col, across < down)
        )
        rank = jnp.sum(before.astype(jnp.int32), axis=1, keepdims=True)
        placed = rank == across
        order_v[0:1, :] = jnp.sum(jnp.where(placed, down, 0), axis=0, keepdims=True)
        order_v[1:2, :] = jnp.sum(jnp.where(placed, key_col, 0), axis=0, keepdims=True)
        order_v[2:3, :] = jnp.sum((key_col <= across).astype(jnp.int32), axis=0, keepdims=True)
        order_v[3:4, :] = jnp.sum((key_col == across).astype(jnp.int32), axis=0, keepdims=True)
        order_v[4:8, :] = jnp.zeros((4, total_slots), jnp.int32)
        order_copy().start()

    def order_copy():
        return pltpu.make_async_copy(order_v, order, load_sem.at[11])

    def relay(k):
        for s in range(2):
            for way in (0, 1):
                if not on_route(way, k, s):
                    continue
                arrival(way, 0, k, s).wait_recv()
                if k == 2:
                    hop(way, 0, 3, s).start()
                    if s == way:
                        hop(way, 0, 4, s).start()
                hop(way, 1, k, s).start()

    def take(k, col):
        for s in range(2):
            for way in (0, 1):
                if on_route(way, k, s):
                    arrival(way, col, k, s).wait_recv()

    def multiply_at(k, col):
        if k in (0, FAR):
            multiply_some([loop_node(k, col)])
        else:
            multiply_some([loop_node(k, col), loop_node(-k, col)])

    multiply_at(0, 0)
    for s in range(2):
        pair(s, 1).wait_recv()
        for way in (0, 1):
            hop(way, 1, 1, s).start()
    relay(2)
    multiply_at(0, 1)
    take(1, 0)
    multiply_at(1, 0)
    take(1, 1)
    multiply_at(1, 1)
    relay(3)
    relay(4)
    base[...] = (
        jnp.dot(x_ref[...], ws_ref[...], preferred_element_type=F32) + bias_ref[...]
    )
    sort_slots()
    pl.semaphore_wait(second_sem, 2)
    for other in (left_chip, right_chip):
        greet(third_sem, (loop, other * 2 + core))
    multiply_at(2, 0)
    multiply_at(3, 0)
    multiply_at(4, 0)
    for k in (2, 3, 4):
        take(k, 1)
        multiply_at(k, 1)
    order_copy().wait()
    pl.semaphore_wait(third_sem, 2)

    def accumulate(i, total):
        for u in range(8):
            j = i * 8 + u
            same = jnp.logical_and(j > 0, order[1, j] == order[1, jnp.maximum(j - 1, 0)])
            total = total * jnp.where(same, 1.0, 0.0) + prod[order[0, j]]
            run[j] = total.astype(BF16)
        return total

    lax.fori_loop(0, total_slots // 8, accumulate, jnp.zeros((blk, blk), F32))

    steps = CHIP_STEPS + ((0, 0),)

    def collect(side, i):
        for s in range(2):
            which = core if side == 0 else 1 - core
            d = (chip_node(*steps[i]) * 2 + which) * 2 + s
            part[side, i, s * blk : (s + 1) * blk, :] = run[
                jnp.where(order[3, d] > 0, order[2, d] - 1, total_slots)
            ]

    def core_copy(i):
        return remote(
            part.at[1, i], core_in.at[i], core_sem.at[0, i], core_sem.at[1, i], mate
        )

    def chip_copy(i):
        return remote(
            chip_out.at[i],
            chip_in.at[i],
            chip_sem.at[0, i],
            chip_sem.at[1, i],
            (loop, chip_node(*steps[i]) * 2 + core),
        )

    for i in range(len(steps)):
        collect(1, i)
        if i > 0:
            core_copy(i - 1).start()
    last = len(steps) - 1
    collect(0, 0)
    core_copy(last).start()
    for i in range(last):
        collect(0, i + 1)
        core_copy(i).wait_recv()
        both = part[0, i].astype(F32) + core_in[i].astype(F32)
        chip_out[i] = both.astype(BF16)
        if i > 0:
            chip_copy(i - 1).start()
    core_copy(last).wait_recv()
    total = part[0, last].astype(F32) + core_in[last].astype(F32)
    chip_copy(last - 1).start()
    for i in reversed(range(last)):
        chip_copy(i).wait_recv()
        total = total + chip_in[i].astype(F32)

    deg_rows = deg_ref[...].astype(F32)
    deg_cols = jnp.concatenate(
        [
            jnp.transpose(jnp.broadcast_to(deg_rows[s : s + 1, :], (blk, blk)))
            for s in range(2)
        ],
        axis=0,
    )
    aggregate = (total / deg_cols).astype(BF16)
    preact = base[...] + jnp.dot(aggregate, wn_ref[...], preferred_element_type=F32)
    sigmoid_val = jax.nn.sigmoid(preact)
    grad_pre = (
        cot_ref[...].astype(F32) * sigmoid_val * (1.0 + preact * (1.0 - sigmoid_val))
    ).astype(BF16)
    out_ref[...] = (preact * sigmoid_val).astype(BF16)
    back = lax.dot_general(
        wn_ref[...], grad_pre, (((1,), (1,)), ((), ())), preferred_element_type=F32
    )
    for s in range(2):
        gt[rep * 2 + s] = (back[:, s * blk : (s + 1) * blk] / deg_rows[s : s + 1, :]).astype(BF16)
    self_grad[...] = lax.dot_general(
        grad_pre, ws_ref[...], (((1,), (1,)), ((), ())), preferred_element_type=F32
    )

    def gather_copy(i):
        dy, dx = CHIP_STEPS[i]
        mine = gt.at[pl.ds(rep * 2, 2)]
        return remote(
            mine,
            mine,
            gath_sem.at[0, i],
            gath_sem.at[1, i],
            (loop, chip_node(dy, dx) * 2 + core),
        )

    def gathered(i):
        dy, dx = CHIP_STEPS[i]
        origin = chip_node((2 - dy) % 2, (X - dx) % X) * 2 + core
        return gt.at[pl.ds(origin * 2, 2)]

    def forward_copy(i):
        block = gathered(i) if i < len(CHIP_STEPS) else gt.at[pl.ds(rep * 2, 2)]
        return remote(block, block, fwd_sem.at[0, i], fwd_sem.at[1, i], mate)

    for i in range(len(CHIP_STEPS)):
        gather_copy(i).start()
    forward_copy(len(CHIP_STEPS)).start()

    wself = lax.dot_general(
        x_ref[...], grad_pre, (((0,), (0,)), ((), ())), preferred_element_type=F32
    )
    wneigh = lax.dot_general(
        aggregate, grad_pre, (((0,), (0,)), ((), ())), preferred_element_type=F32
    )
    wbias = jnp.sum(grad_pre.astype(F32), axis=0, keepdims=True)
    for j in range(8):
        wpart[j, 0:16, :] = wself[16 * j : 16 * j + 16, :]
        wpart[j + 8, 0:16, :] = wneigh[16 * j : 16 * j + 16, :]
        wpart[j, 16:24, :] = jnp.broadcast_to(wbias, (8, wbias.shape[1]))
        wpart[j + 8, 16:24, :] = jnp.broadcast_to(wbias, (8, wbias.shape[1]))
    piece = core * 8 + chip

    def w1_mate():
        return remote(
            wpart.at[pl.ds((1 - core) * 8, 8)], wmate, w1_sem.at[0, 7], w1_sem.at[1, 7], mate
        )

    def w1_copy(i, sending):
        dy, dx = CHIP_STEPS[i]
        slot = chip if sending else chip_node((2 - dy) % 2, (X - dx) % X)
        to = chip_node(dy, dx)
        return remote(
            wpart.at[core * 8 + to],
            win.at[slot],
            w1_sem.at[0, i],
            w1_sem.at[1, i],
            (loop, to * 2 + core),
        )

    def w2_copy(stage, j, sending):
        step = 4**stage
        own = loop // step % 4
        to = loop + (lax.rem(own + j, 4) - own) * step
        slot = own if sending else lax.rem(own + 4 - j, 4)
        block = rows_in.at[stage, slot]
        return remote(
            block, block, w2_sem.at[0, stage, j], w2_sem.at[1, stage, j], (to, rep)
        )

    def w2_send(stage, value):
        rows_in[stage, loop // 4**stage % 4] = value
        for j in range(1, 4):
            pending.append(w2_copy(stage, j, True))

    def w2_sum(stage):
        for j in range(1, 4):
            w2_copy(stage, j, False).wait_recv()
        value = rows_in[stage, 0]
        for j in range(1, 4):
            value = value + rows_in[stage, j]
        return value

    def w3_copy(i, sending):
        dy, dx = CHIP_STEPS[i]
        slot = chip if sending else chip_node((2 - dy) % 2, (X - dx) % X)
        block = wfull.at[core * 8 + slot]
        return remote(
            block,
            block,
            w3_sem.at[0, i],
            w3_sem.at[1, i],
            (loop, chip_node(dy, dx) * 2 + core),
        )

    def w3_mate(side):
        block = wfull.at[pl.ds(side * 8, 8)]
        return remote(block, block, w3_sem.at[0, 7], w3_sem.at[1, 7], mate)

    w1_mate().start()
    for i in reversed(range(len(CHIP_STEPS))):
        block = gathered(i)
        remote(
            block, block, gath_sem.at[0, i], gath_sem.at[1, i], mate
        ).wait_recv()
        forward_copy(i).start()
        if i == 4:
            w1_mate().wait_recv()
            for j in range(8):
                wpart[core * 8 + j] = wpart[core * 8 + j] + wmate[j]
            win[chip] = wpart[piece]
        if i == 3:
            for j in range(len(CHIP_STEPS)):
                w1_copy(j, True).start()
    for i in range(len(CHIP_STEPS) + 1):
        if i < len(CHIP_STEPS):
            dy, dx = CHIP_STEPS[i]
            origin = chip_node((2 - dy) % 2, (X - dx) % X) * 2 + (1 - core)
        else:
            origin = chip * 2 + (1 - core)
        block = gt.at[pl.ds(origin * 2, 2)]
        remote(block, block, fwd_sem.at[0, i], fwd_sem.at[1, i], mate).wait_recv()

    def compute(count, k, first):
        def body(j, carry):
            if k in (0, FAR):
                q = loop_node(k, 1 - j)
            else:
                q = loop_node(k * (1 - 2 * (j % 2)), 1 - j // 2)
            sums = [jnp.zeros((blk, blk), F32) for _ in range(2)]
            for t in range(slots):
                d = jnp.where(t < live_ref[0, q], dst_ref[q, t], blocks)
                value = jnp.dot(
                    gt[d], tile_ref[q, t * blk : (t + 1) * blk, :], preferred_element_type=F32
                )
                for s in range(2):
                    sums[s] = sums[s] + value * jnp.where(src_ref[q, t] == s, 1.0, 0.0)
            for s in range(2):
                term[first + j, s * blk : (s + 1) * blk, :] = sums[s]
            return carry

        lax.fori_loop(0, count, body, 0)

    def ring_copy(way, col, k, s):
        rows = pl.ds(s * blk, blk)
        return remote(
            ring_out.at[way, col, k - 1, rows],
            ring_in.at[way, col, k - 1, rows],
            ring_sem.at[0, way, col, k - 1, s],
            ring_sem.at[1, way, col, k - 1, s],
            (loop_node((1 - 2 * way) * STRIDE[k], 0), rep),
        )

    pending = []

    def launch(copy):
        while pending:
            pending.pop(0).start()
        if copy is not None:
            pending.append(copy)

    def ring_send(k, first, cols):
        for col in cols:
            for s in range(2):
                rows = slice(s * blk, (s + 1) * blk)
                for way in (0, 1):
                    if not on_route(way, k, s):
                        continue
                    j = first + (1 - col if k == FAR else (1 - col) * 2 + way)
                    value = term[j, rows, :]
                    if k == 2:
                        ring_copy(way, col, 3, s).wait_recv()
                        value = value + ring_in[way, col, 2, rows, :].astype(F32)
                        if s == way:
                            ring_copy(way, col, 4, s).wait_recv()
                            value = value + ring_in[way, col, 3, rows, :].astype(F32)
                    ring_out[way, col, k - 1, rows, :] = value.astype(BF16)
                    launch(ring_copy(way, col, k, s))

    compute(4, 3, 0)
    ring_send(3, 0, (1, 0))
    for i in reversed(range(len(CHIP_STEPS))):
        w1_copy(i, False).wait_recv()
    value = win[0]
    for j in range(1, 8):
        value = value + win[j]
    w2_send(0, value)
    compute(2, FAR, 4)
    ring_send(FAR, 4, (1, 0))
    launch(None)
    compute(4, 2, 0)
    compute(4, 1, 4)
    w2_send(1, w2_sum(0))
    ring_send(1, 4, (1,))
    ring_send(2, 0, (1,))
    ring_send(1, 4, (0,))
    ring_send(2, 0, (0,))
    launch(None)
    grad_scale = 1.0 / math.sqrt(x_ref.shape[0] * peers * peers)
    value = w2_sum(1)
    gb_ref[...] = value[16:17, :] * grad_scale
    wfull[piece] = value[0:16, :] * grad_scale
    compute(2, 0, 0)
    for i in range(len(CHIP_STEPS)):
        w3_copy(i, True).start()

    def arrived(col, s):
        rows = slice(s * blk, (s + 1) * blk)
        value = term[1 - col, rows, :]
        for way in (0, 1):
            for k in (1, 2):
                ring_copy(way, col, k, s).wait_recv()
                value = value + ring_in[way, col, k - 1, rows, :].astype(F32)
        return value

    def col_copy(s):
        rows = pl.ds(s * blk, blk)
        return remote(
            col_out.at[rows],
            col_in.at[rows],
            col_sem.at[0, s],
            col_sem.at[1, s],
            (loop_node(0, 1), rep),
        )

    for s in range(2):
        col_out[s * blk : (s + 1) * blk, :] = arrived(1, s).astype(BF16)
        if s == 1:
            col_copy(0).start()
    mine = [arrived(0, 0)]
    col_copy(1).start()
    mine.append(arrived(0, 1))
    for i in reversed(range(len(CHIP_STEPS))):
        w3_copy(i, False).wait_recv()
    w3_mate(core).start()
    for s in range(2):
        rows = slice(s * blk, (s + 1) * blk)
        col_copy(s).wait_recv()
        value = mine[s] + col_in[rows, :].astype(F32)
        gin_ref[rows, :] = (self_grad[rows, :] + jnp.transpose(value)).astype(BF16)
    w3_mate(1 - core).wait_recv()
    for j in range(8):
        gs_ref[16 * j : 16 * j + 16, :] = wfull[j]
        gn_ref[16 * j : 16 * j + 16, :] = wfull[j + 8]

    for s in range(2):
        pair(s, 0).wait_send()
        col_copy(s).wait_send()
    for i in range(len(steps)):
        core_copy(i).wait_send()
        forward_copy(i).wait_send()
    for i in range(len(CHIP_STEPS)):
        chip_copy(i).wait_send()
        gather_copy(i).wait_send()
    for k in range(1, FAR + 1):
        for col in (0, 1):
            for s in range(2):
                for way in (0, 1):
                    if on_route(way, k, s):
                        hop(way, col, k, s).wait_send()
                        ring_copy(way, col, k, s).wait_send()
    for i in range(len(CHIP_STEPS)):
        w1_copy(i, True).wait_send()
        w3_copy(i, True).wait_send()
    for stage in range(2):
        for j in range(1, 4):
            w2_copy(stage, j, True).wait_send()
    w1_mate().wait_send()
    w3_mate(core).wait_send()


def finish_kernel(*refs):
    for a, b in zip(refs[:5], refs[5:]):
        b[...] = a[...]


def per_device(
    features, w_self, w_neigh, bias, degree, tiles, dst_block, src_block, live_count, cotangent
):
    rows, feat = features.shape
    hidden = w_self.shape[1]
    sources, slots, blk = tiles.shape[2], tiles.shape[3], tiles.shape[4]
    blocks = 2 * 16
    vmem = pl.BlockSpec(memory_space=pltpu.VMEM)
    hbm = pl.BlockSpec(memory_space=pl.ANY)
    dma = pltpu.SemaphoreType.DMA
    shape = jax.ShapeDtypeStruct
    smem = pltpu.SMEM

    results = (
        shape((rows, hidden), BF16),
        shape((rows, feat), BF16),
        shape((feat, hidden), F32),
        shape((feat, hidden), F32),
        shape((1, hidden), F32),
    )
    made = pl.pallas_call(
        layer_kernel,
        out_shape=results,
        in_specs=[hbm] * 10,
        out_specs=(vmem,) * 5,
        scratch_shapes=[
            smem((sources, slots), jnp.int32),
            smem((sources, slots), jnp.int32),
            smem((1, sources), jnp.int32),
            pltpu.VMEM((sources, slots), jnp.int32),
            pltpu.VMEM((1, sources), jnp.int32),
            pltpu.VMEM((rows, feat), BF16),
            pltpu.VMEM((feat, hidden), BF16),
            pltpu.VMEM((feat, hidden), BF16),
            pltpu.VMEM((1, hidden), F32),
            pltpu.VMEM((rows // blk, blk), jnp.int32),
            pltpu.VMEM((rows, hidden), BF16),
            pltpu.VMEM((sources, slots * blk, blk), BF16),
            pltpu.VMEM((sources * 2, blk, feat), BF16),
            pltpu.VMEM((2, blk, feat), BF16),
            pltpu.VMEM((sources * slots, blk, feat), F32),
            pltpu.VMEM((sources * slots + 1, blk, feat), BF16),
            pltpu.VMEM((8, sources * slots), jnp.int32),
            smem((8, sources * slots), jnp.int32),
            pltpu.VMEM((2, 8, rows, feat), BF16),
            pltpu.VMEM((8, rows, feat), BF16),
            pltpu.VMEM((7, rows, feat), BF16),
            pltpu.VMEM((7, rows, feat), BF16),
            pltpu.VMEM((blocks + 1, feat, blk), BF16),
            pltpu.VMEM((8, 2 * feat, blk), F32),
            pltpu.VMEM((rows, hidden), F32),
            pltpu.VMEM((rows, feat), F32),
            pltpu.VMEM((2, 2, FAR, 2 * feat, blk), BF16),
            pltpu.VMEM((2, 2, FAR, 2 * feat, blk), BF16),
            pltpu.VMEM((2 * feat, blk), BF16),
            pltpu.VMEM((2 * feat, blk), BF16),
            pltpu.VMEM((16, 24, hidden), F32),
            pltpu.VMEM((8, 24, hidden), F32),
            pltpu.VMEM((2, 4, 24, hidden), F32),
            pltpu.VMEM((8, 24, hidden), F32),
            pltpu.VMEM((16, 16, hidden), F32),
            dma((sources,)),
            dma((12,)),
            dma((2, 2)),
            dma((2, 2, 2, FAR, 2)),
            dma((2, 8)),
            dma((2, 7)),
            dma((2, 7)),
            dma((2, 8)),
            dma((2, 2, 2, FAR, 2)),
            dma((2, 2)),
            dma((2, 8)),
            dma((2, 2, 4)),
            dma((2, 8)),
            pltpu.SemaphoreType.REGULAR,
            pltpu.SemaphoreType.REGULAR,
        ],
        compiler_params=pltpu.CompilerParams(
            collective_id=0, has_side_effects=True, vmem_limit_bytes=57 << 20
        ),
        name="layer",
    )(
        dst_block.reshape(sources, slots),
        src_block.reshape(sources, slots),
        live_count.reshape(1, sources),
        features,
        w_self,
        w_neigh,
        bias.reshape(1, hidden),
        degree.reshape(rows // blk, blk),
        cotangent,
        tiles.reshape(sources, slots * blk, blk),
    )
    output, grad_input, grad_self, grad_neigh, grad_bias = pl.pallas_call(
        finish_kernel,
        out_shape=results,
        in_specs=[vmem] * 5,
        out_specs=(vmem,) * 5,
        name="finish",
    )(*made)
    return output, grad_input, grad_self, grad_neigh, grad_bias.reshape(hidden)


def solution(mesh):
    in_specs = (
        P(("loop", "rep"), None),
        P(),
        P(),
        P(),
        P(("loop", "rep")),
        P("loop", "rep", None, None, None, None),
        P("loop", "rep", None, None),
        P("loop", "rep", None, None),
        P("loop", "rep", None),
        P(("loop", "rep"), None),
    )
    out_specs = (P(("loop", "rep"), None), P(("loop", "rep"), None), P(), P(), P())
    return jax.shard_map(
        per_device, mesh=mesh, in_specs=in_specs, out_specs=out_specs, check_vma=False
    )
```
